32 devices in a mesh: survey: 2 (over y), band: 4 (over z), role: 4 (over x, core).
Axes of the slice: x: 2, y: 2, z: 4, core: 2. Of those that a mesh axis runs over, the one named last changes fastest.
Arguments:
- vel_index: int32 [16, 32, 128], P('role', 'band'), may hold values from 0 to 31
- courant: float32 [32], replicated, may hold values from 0.05 to 0.19
- src_now: float32 [32, 32, 128], P(('survey', 'role'), 'band'), parts along dimension 0, may hold values from -4 to 4
- src_prev: float32 [32, 32, 128], P(('survey', 'role'), 'band'), parts along dimension 0, may hold values from -4 to 4
- rec_now: float32 [32, 32, 128], P(('survey', 'role'), 'band'), parts along dimension 0, may hold values from -4 to 4
- rec_prev: float32 [32, 32, 128], P(('survey', 'role'), 'band'), parts along dimension 0, may hold values from -4 to 4
- src_pos: int32 [8, 3], P('survey'), parts along dimension 0, may hold values from 0 to 127, as said below
- src_wavelet: float32 [8, 16], P('survey'), parts along dimension 0, may hold values from -16 to 16
- rec_pos: int32 [8192, 2], P('survey'), parts along dimension 0, may hold values from 0 to 127, as said below
- rec_traces: float32 [8192, 16], P('survey'), parts along dimension 0, may hold values from -16 to 16
- offset_lags: int32 [32], replicated, may hold values from -16 to 16, as said below
Outputs:
- image: bfloat16 [64, 16, 32, 128], P('survey', 'role', 'band'), parts along dimension 0
- src_final: float32 [32, 32, 128], P(('survey', 'role'), 'band'), parts along dimension 0
- rec_final: float32 [32, 32, 128], P(('survey', 'role'), 'band'), parts along dimension 0
The draws below stay inside these ranges and needn't reach their ends.
There are 2 independent parts, one for each index of `survey`. The reference program is written for one: setup_inputs(seed, part) draws one part's arguments, and reference() takes and returns one part's arrays. A program takes and returns all parts, laid end to end along the dimension named above; an argument that names none is the same for every part. Nothing has to cross between parts.
Inputs may be any that keep to these rules, and one draw needn't show every extreme that they name: `src_pos`: column 0 is a depth cell below 16, column 1 a cross-line cell below 32, column 2 an inline cell below 128; sources may share cells. `rec_pos`: column 0 is a cross-line cell below 32, column 1 an inline cell below 128; receivers may share cells. `offset_lags`: increasing and distinct: every whole number from -16 to 16 except one of the interior ones.
All inputs are finite; a program needn't handle non-finite values.
Results may differ from the reference program's by a relative error of at most 0.004.
Values may be sent and summed in bfloat16 or wider, within the bound.
No kernel may reach another device: no remote copies, remote signals or barrier semaphores. Data moves between devices by JAX's collectives and lax.ppermute only.
A program may use at most 128 MiB of HBM per device.

```python
import jax
import jax.numpy as jnp
from jax import lax

NLAG = 32
LEVELS = 32
SUB = 4
IMAGES = 4
NSRC = 4
NREC = 4096
STEPS = 16
NZ = 16
NY = 32
NX = 128


def draw_positions(key, row_count, limits, forced):
    columns = []
    for column, upper in enumerate(limits):
        columns.append(jax.random.randint(jax.random.fold_in(key, column), (row_count,), 0, upper))
    coords = jnp.stack(columns, axis=1).astype(jnp.int32)
    for row_at, column, set_value in forced:
        coords = coords.at[row_at, column].set(set_value)
    return coords


def draw_src_pos(key, part):
    return draw_positions(jax.random.fold_in(key, 11), NSRC, (NZ, NY, NX), ((0, 2, NX - 1), (1, 1, NY - 1), (2, 0, NZ - 1)))


def draw_rec_pos(key, part):
    return draw_positions(jax.random.fold_in(key, 12), NREC, (NY, NX), ((0, 1, NX - 1), (1, 0, NY - 1)))


def draw_offset_lags(key, part):
    half_span = NLAG // 2
    missing = jax.random.randint(jax.random.fold_in(key, 13), (), 1 - half_span, half_span)
    ordered = jnp.arange(NLAG, dtype=jnp.int32) - half_span
    return (ordered + (ordered >= missing).astype(jnp.int32)).astype(jnp.int32)


def place_ends(entries, key, least, top_value):
    index_at = [jax.random.randint(jax.random.fold_in(key, axis), (), 0, length) for axis, length in enumerate(entries.shape)]
    widest = entries.shape.index(max(entries.shape))
    next_to = index_at[:widest] + [(index_at[widest] + 1) % entries.shape[widest]] + index_at[widest + 1:]
    return entries.at[tuple(index_at)].set(least).at[tuple(next_to)].set(top_value)


def levels(key, dims, pieces, smallest, top_value):
    def one(axis_at, blocks):
        heights = jax.random.uniform(jax.random.fold_in(jax.random.fold_in(key, 6), axis_at), (blocks,), jnp.float32, smallest / len(pieces), top_value / len(pieces))
        return jnp.repeat(jnp.exp(heights), dims[axis_at] // blocks).reshape((-1,) + (1,) * (len(dims) - axis_at - 1))

    level = one(*pieces[0])
    for cut in pieces[1:]:
        level = level * one(*cut)
    return level


def scatter_about(stream_key, extent, deviation, bound, shards=(), held_as=jnp.bfloat16):
    drawn = deviation * jax.random.normal(stream_key, extent, jnp.float32)
    if shards:
        drawn = drawn * levels(stream_key, extent, shards, -0.22, 0.18)
    return jnp.clip(drawn, -bound, bound).astype(held_as)


def setup_inputs(seed: int = 0, part: int = 0) -> dict:
    seeds = jax.random.split(jax.random.key(seed), 12)
    own_keys = jax.random.split(jax.random.fold_in(seeds[11], part), 12)
    vel_index = place_ends(jax.random.randint(seeds[0], (NZ, NY, NX), 0, LEVELS), jax.random.fold_in(seeds[0], 1), 0, LEVELS - 1).astype(jnp.int32)
    courant = jnp.clip(jax.random.uniform(seeds[1], (LEVELS,), jnp.float32, 0.05, 0.19), 0.05, 0.19)
    src_now = scatter_about(own_keys[2], (NZ, NY, NX), 0.5, 4.0, ((0, 4), (1, 4)), jnp.float32)
    src_prev = scatter_about(own_keys[3], (NZ, NY, NX), 0.5, 4.0, ((0, 4), (1, 4)), jnp.float32)
    rec_now = scatter_about(own_keys[4], (NZ, NY, NX), 0.5, 4.0, ((0, 4), (1, 4)), jnp.float32)
    rec_prev = scatter_about(own_keys[5], (NZ, NY, NX), 0.5, 4.0, ((0, 4), (1, 4)), jnp.float32)
    src_pos = draw_src_pos(jax.random.fold_in(jax.random.fold_in(seeds[11], part), 71), part)
    src_wavelet = scatter_about(own_keys[7], (NSRC, STEPS), 4.0, 16.0, (), jnp.float32)
    rec_pos = draw_rec_pos(jax.random.fold_in(jax.random.fold_in(seeds[11], part), 71), part)
    rec_traces = scatter_about(own_keys[9], (NREC, STEPS), 4.0, 16.0, (), jnp.float32)
    offset_lags = draw_offset_lags(jax.random.fold_in(seeds[11], 71), part)
    return dict(vel_index=vel_index, courant=courant, src_now=src_now, src_prev=src_prev, rec_now=rec_now, rec_prev=rec_prev, src_pos=src_pos, src_wavelet=src_wavelet, rec_pos=rec_pos, rec_traces=rec_traces, offset_lags=offset_lags)


STENCIL_WEIGHTS = (-205.0 / 72.0, 8.0 / 5.0, -1.0 / 5.0, 8.0 / 315.0, -1.0 / 560.0)


def laplace(field):
    depth_cells, row_cells, col_cells = field.shape
    padded = jnp.pad(field, 4)

    def window(along_z, along_y, along_x):
        return padded[4 + along_z:4 + along_z + depth_cells, 4 + along_y:4 + along_y + row_cells, 4 + along_x:4 + along_x + col_cells]

    summed = (3.0 * STENCIL_WEIGHTS[0]) * field
    for distance in range(1, 5):
        weight = STENCIL_WEIGHTS[distance]
        pairs = window(distance, 0, 0) + window(-distance, 0, 0)
        pairs = pairs + window(0, distance, 0) + window(0, -distance, 0)
        pairs = pairs + window(0, 0, distance) + window(0, 0, -distance)
        summed = summed + weight * pairs
    return summed


def inject(shape, depth_at, row_at, col_at, amounts):
    return jnp.zeros(shape, jnp.float32).at[depth_at, row_at, col_at].add(amounts)


def reference(vel_index, courant, src_now, src_prev, rec_now, rec_prev, src_pos, src_wavelet, rec_pos, rec_traces, offset_lags):
    speed = courant[vel_index]
    shape = src_now.shape
    source, source_old = src_now, src_prev
    receiver, receiver_old = rec_now, rec_prev
    max_lag = NLAG // 2
    image_sum = jnp.zeros((NLAG,) + shape, jnp.float32)
    rec_depth = jnp.zeros_like(rec_pos[:, 0])
    for snapshot in range(IMAGES):
        for substep in range(SUB):
            tick_at = snapshot * SUB + substep
            source_term = inject(shape, src_pos[:, 0], src_pos[:, 1], src_pos[:, 2], src_wavelet[:, tick_at])
            receiver_term = inject(shape, rec_depth, rec_pos[:, 0], rec_pos[:, 1], rec_traces[:, tick_at])
            source_new = 2.0 * source - source_old + speed * (laplace(source) + source_term)
            receiver_new = 2.0 * receiver - receiver_old + speed * (laplace(receiver) + receiver_term)
            source_old, source = source, source_new
            receiver_old, receiver = receiver, receiver_new
        source_pad = jnp.pad(source, ((0, 0), (0, 0), (max_lag, max_lag)))
        receiver_pad = jnp.pad(receiver, ((0, 0), (0, 0), (max_lag, max_lag)))

        def add_lag(lag_slot, summed):
            lag_value = offset_lags[lag_slot]
            src_part = lax.dynamic_slice_in_dim(source_pad, (max_lag - lag_value).astype(jnp.int32), NX, 2)
            rec_part = lax.dynamic_slice_in_dim(receiver_pad, (max_lag + lag_value).astype(jnp.int32), NX, 2)
            return summed.at[lag_slot].add(src_part * rec_part)

        image_sum = lax.fori_loop(0, NLAG, add_lag, image_sum)
    padded = jnp.pad(image_sum, ((0, 0), (1, 1), (0, 0), (0, 0)))
    depth_cells = shape[0]
    filtered = 2.0 * padded[:, 1:1 + depth_cells] - padded[:, 0:depth_cells] - padded[:, 2:2 + depth_cells]
    return filtered.astype(jnp.bfloat16), source, receiver
```

```python
import functools

import jax
import jax.numpy as jnp
from jax import lax
from jax.experimental import pallas as pl
from jax.experimental.pallas import tpu as pltpu
from jax.sharding import PartitionSpec as P

SUB = 4
IMAGES = 4
PARTS = 5
CORES = 2

STENCIL_WEIGHTS = (-205.0 / 72.0, 8.0 / 5.0, -1.0 / 5.0, 8.0 / 315.0, -1.0 / 560.0)
F32 = jnp.float32
BF16 = jnp.bfloat16

VMEM_SPEC = pl.BlockSpec(memory_space=pltpu.VMEM)
SMEM_SPEC = pl.BlockSpec(memory_space=pltpu.SMEM)


def split(value):
    high = value.astype(BF16)
    return high, (value - high.astype(F32)).astype(BF16)


def pack_kernel(vel_ref, sn_ref, sp_ref, rn_ref, rp_ref, keep_ref, send_ref):
    core = lax.rem(lax.axis_index("role"), CORES)
    entry = vel_ref[...].astype(F32).astype(BF16)
    src_now, rec_now = sn_ref[...], rn_ref[...]
    src_step, rec_step = src_now - sp_ref[...], rec_now - rp_ref[...]
    for out_ref, wants_source in ((keep_ref, core == 0), (send_ref, core != 0)):
        now = jnp.where(wants_source, src_now, rec_now)
        step = jnp.where(wants_source, src_step, rec_step)
        out_ref[0], out_ref[1] = split(now)
        out_ref[2], out_ref[3] = split(step)
        out_ref[4] = entry


def pack(vel_index, src_now, src_prev, rec_now, rec_prev):
    shape = jax.ShapeDtypeStruct((PARTS,) + src_now.shape, BF16)
    return pl.pallas_call(
        pack_kernel,
        out_shape=(shape, shape),
        in_specs=[VMEM_SPEC] * 5,
        out_specs=(VMEM_SPEC, VMEM_SPEC),
        name="pack",
    )(vel_index, src_now, src_prev, rec_now, rec_prev)


def inject_kernel(chunk, pos_ref, amp_ref, out_ref, acc_ref):
    steps, count = amp_ref.shape
    _, rows, cols = out_ref.shape
    acc_ref[...] = jnp.zeros_like(acc_ref)

    def one(at, carry):
        span = pl.ds(pl.multiple_of(at * chunk, chunk), chunk)
        pos = pos_ref[:, span]
        in_row = lax.broadcasted_iota(jnp.int32, (rows, chunk), 0) == pos[0:1]
        in_col = lax.broadcasted_iota(jnp.int32, (cols, chunk), 0) == pos[1:2]
        col_hot = jnp.where(in_col, 1.0, 0.0).astype(BF16)
        amp = amp_ref[:, span]
        high = amp.astype(BF16).astype(F32)
        total = None
        for part in (high, amp - high):
            spread = jnp.concatenate(
                [jnp.where(in_row, part[k : k + 1], 0.0).astype(BF16) for k in range(steps)], axis=0
            )
            added = lax.dot_general(
                spread, col_hot, (((1,), (1,)), ((), ())), preferred_element_type=F32
            )
            total = added if total is None else total + added
        acc_ref[...] += total
        return carry

    lax.fori_loop(0, count // chunk, one, 0)
    for k in range(steps):
        out_ref[k] = acc_ref[k * rows : (k + 1) * rows]


def inject(rec_pos, rec_traces, rows, cols):
    count, steps = rec_traces.shape
    chunk = next(c for c in (512, 256, 128, count) if count % c == 0)
    return pl.pallas_call(
        functools.partial(inject_kernel, chunk),
        out_shape=jax.ShapeDtypeStruct((steps, rows, cols), F32),
        in_specs=[VMEM_SPEC] * 2,
        out_specs=VMEM_SPEC,
        scratch_shapes=[pltpu.VMEM((steps * rows, cols), F32)],
        name="inject",
    )(rec_pos.T, rec_traces.T)


def lookup(table, entry):
    width = table.shape[1]
    pieces = [
        jnp.take_along_axis(table, entry[:, at : at + width], axis=1)
        for at in range(0, entry.shape[1], width)
    ]
    return pieces[0] if len(pieces) == 1 else jnp.concatenate(pieces, axis=1)


def step_kernel(bands, chips, steps, *refs):
    wavelet_ref, src_pos_ref, table_ref, added_ref = refs[:4]
    piece_refs = refs[4 : 4 + bands * chips]
    keep_ref, send_ref, one_ref, two_ref, speed_ref, row_ref = refs[4 + bands * chips :]
    _, _, tile_z, tile_y, cols = piece_refs[0].shape
    depth, rows, _ = speed_ref.shape
    role, band = lax.axis_index("role"), lax.axis_index("band")
    core, chip = lax.rem(role, CORES), lax.div(role, CORES)
    is_source = core == 0
    sources = src_pos_ref.shape[0]

    for ref in (one_ref, two_ref):
        edge = jnp.zeros((rows + 16, cols), F32)
        ref[0] = edge
        ref[depth + 1] = edge
        for z in range(1, depth + 1):
            ref[z, 0:8] = edge[0:8]
            ref[z, rows + 8 :] = edge[0:8]

    table = jnp.broadcast_to(table_ref[...], (tile_y, table_ref.shape[1]))
    for shift in range(bands):
        from_band = lax.rem(band + (bands - shift), bands)
        y0 = pl.multiple_of(from_band * tile_y, tile_y)
        for hop in range(chips):
            from_chip = lax.rem(chip + (chips - hop), chips)
            piece = piece_refs[shift * chips + hop]
            for part in range(CORES):
                from_core = core if part == 0 else 1 - core
                z0 = (from_chip * CORES + from_core) * tile_z
                for z in range(tile_z):
                    planes = [piece[part, k, z].astype(F32) for k in range(PARTS)]
                    now = planes[0] + planes[1]
                    one_ref[z0 + z + 1, pl.ds(y0 + 8, tile_y)] = now
                    two_ref[z0 + z + 1, pl.ds(y0 + 8, tile_y)] = now - (planes[2] + planes[3])
                    speed_ref[z0 + z, pl.ds(y0, tile_y)] = lookup(table, planes[4].astype(jnp.int32))

    lane = lax.broadcasted_iota(jnp.int32, (1, cols), 1)
    for i in range(sources):
        speed_row = speed_ref[src_pos_ref[i, 0], pl.ds(src_pos_ref[i, 1], 1)]
        row_ref[pl.ds(i, 1)] = jnp.where(lane == src_pos_ref[i, 2], speed_row, 0.0)

    lanes = lax.broadcasted_iota(jnp.int32, (8, cols), 1)
    low_side, high_side = [], []
    for j in range(1, 5):
        low_side.append(jnp.where(lanes >= j, STENCIL_WEIGHTS[j], 0.0))
        high_side.append(jnp.where(lanes < cols - j, STENCIL_WEIGHTS[j], 0.0))

    def beside(ref, z, y0, distance):
        if isinstance(y0, int):
            return ref[z + 1, pl.ds(y0 + 8 + distance, 8)]
        return ref[z + 1, pl.ds(y0, 24)][8 + distance : 16 + distance]

    def stencil_rows(now_ref, new_ref, y0):
        mids = [None] * 4 + [now_ref[z + 1, pl.ds(y0 + 8, 8)] for z in range(4)]
        for z in range(depth):
            mids.append(now_ref[z + 5, pl.ds(y0 + 8, 8)] if z + 4 < depth else None)
            mid = mids[4]
            total = (3.0 * STENCIL_WEIGHTS[0]) * mid
            for j in range(1, 5):
                pairs = beside(now_ref, z, y0, j) + beside(now_ref, z, y0, -j)
                for near in (mids[4 - j], mids[4 + j]):
                    if near is not None:
                        pairs = pairs + near
                total = total + STENCIL_WEIGHTS[j] * pairs
                total = total + low_side[j - 1] * pltpu.roll(mid, j, 1)
                total = total + high_side[j - 1] * pltpu.roll(mid, cols - j, 1)
            mids.pop(0)
            old = new_ref[z + 1, pl.ds(y0 + 8, 8)]
            new_ref[z + 1, pl.ds(y0 + 8, 8)] = (2.0 * mid - old) + speed_ref[z, pl.ds(y0, 8)] * total

    def advance(now_ref, new_ref, tick):
        tiles = rows // 8
        if tiles * depth * cols <= 64 * 128:
            for tile in range(tiles):
                stencil_rows(now_ref, new_ref, tile * 8)
        else:

            def one_tile(tile, carry):
                stencil_rows(now_ref, new_ref, pl.multiple_of(tile * 8, 8))
                return carry

            lax.fori_loop(0, tiles, one_tile, 0)

        @pl.when(is_source)
        def _():
            for i in range(sources):
                at = (src_pos_ref[i, 0] + 1, pl.ds(src_pos_ref[i, 1] + 8, 1))
                new_ref[at] = new_ref[at] + wavelet_ref[i, tick] * row_ref[pl.ds(i, 1)]

        @pl.when(jnp.logical_not(is_source))
        def _():
            new_ref[1, 8 : rows + 8] = new_ref[1, 8 : rows + 8] + speed_ref[0] * added_ref[tick]

    y_own = pl.ds(pl.multiple_of(band * tile_y, tile_y) + 8, tile_y)

    def image_time(snapshot, carry):
        refs_at = (one_ref, two_ref)
        for substep in range(SUB):
            advance(refs_at[substep % 2], refs_at[1 - substep % 2], snapshot * SUB + substep)
        for out_ref, owner in ((keep_ref, role), (send_ref, chip * CORES + (1 - core))):
            for z in range(tile_z + 2):
                out_ref[snapshot, z] = refs_at[SUB % 2][owner * tile_z + z, y_own]
        return carry

    lax.fori_loop(0, steps // SUB, image_time, 0)


def propagate(pieces, bands, chips, wavelet, src_pos, table, added):
    _, _, tile_z, tile_y, cols = pieces[0].shape
    depth, rows = chips * CORES * tile_z, bands * tile_y
    steps = wavelet.shape[1]
    snaps = jax.ShapeDtypeStruct((steps // SUB, tile_z + 2, tile_y, cols), F32)
    field = pltpu.VMEM((depth + 2, rows + 16, cols), F32)
    return pl.pallas_call(
        functools.partial(step_kernel, bands, chips, steps),
        out_shape=(snaps, snaps),
        in_specs=[SMEM_SPEC] * 2 + [VMEM_SPEC] * (2 + len(pieces)),
        out_specs=(VMEM_SPEC, VMEM_SPEC),
        scratch_shapes=[
            field,
            field,
            pltpu.VMEM((depth, rows, cols), F32),
            pltpu.VMEM((max(8, src_pos.shape[0]), cols), F32),
        ],
        name="propagate",
    )(wavelet, src_pos, table, added, *pieces)


def image_kernel(lag_ref, own_ref, other_ref, image_ref, src_ref, rec_ref):
    is_source = lax.rem(lax.axis_index("role"), CORES) == 0
    images, planes, tile_y, cols = own_ref.shape
    source = [[None] * planes for _ in range(images)]
    receiver = [[None] * planes for _ in range(images)]
    for i in range(images):
        for z in range(planes):
            own, other = own_ref[i, z], other_ref[i, z]
            source[i][z] = jnp.where(is_source, own, other)
            receiver[i][z] = jnp.where(is_source, other, own)
    for z in range(planes - 2):
        src_ref[z] = source[images - 1][z + 1]
        rec_ref[z] = receiver[images - 1][z + 1]
    lanes = lax.broadcasted_iota(jnp.int32, (tile_y, cols), 1)
    for slot in range(lag_ref.shape[0]):
        lag = lag_ref[slot]
        reach = jnp.abs(lag)
        there = lax.rem(2 * cols - 2 * lag, cols)
        back = lax.rem(cols + lag, cols)
        sums = []
        for z in range(planes):
            total = None
            for i in range(images):
                term = source[i][z] * pltpu.roll(receiver[i][z], there, 1)
                total = term if total is None else total + term
            sums.append(total)
        inside = (lanes >= reach) & (lanes < cols - reach)
        for z in range(planes - 2):
            value = (2.0 * sums[z + 1] - sums[z]) - sums[z + 2]
            image_ref[slot, z] = jnp.where(inside, pltpu.roll(value, back, 1), 0.0).astype(BF16)


def make_image(lags, own, other):
    _, planes, tile_y, cols = own.shape
    field = jax.ShapeDtypeStruct((planes - 2, tile_y, cols), F32)
    return pl.pallas_call(
        image_kernel,
        out_shape=(
            jax.ShapeDtypeStruct((lags.shape[0], planes - 2, tile_y, cols), BF16),
            field,
            field,
        ),
        in_specs=[SMEM_SPEC] + [VMEM_SPEC] * 2,
        out_specs=(VMEM_SPEC,) * 3,
        name="image",
    )(lags, own, other)


def shards(
    vel_index,
    courant,
    src_now,
    src_prev,
    rec_now,
    rec_prev,
    src_pos,
    src_wavelet,
    rec_pos,
    rec_traces,
    offset_lags,
):
    bands, roles = lax.axis_size("band"), lax.axis_size("role")
    chips = roles // CORES
    cols = src_now.shape[2]
    partner = [(i, i + 1 - 2 * (i % CORES)) for i in range(roles)]

    keep, send = pack(vel_index, src_now, src_prev, rec_now, rec_prev)
    pair = jnp.stack([keep, lax.ppermute(send, "role", partner)])
    pieces = []
    for shift in range(bands):
        moved = pair
        if shift:
            moved = lax.ppermute(pair, "band", [(i, (i + shift) % bands) for i in range(bands)])
        pieces.append(moved)
        for hop in range(1, chips):
            perm = [(i, (i + CORES * hop) % roles) for i in range(roles)]
            pieces.append(lax.ppermute(moved, "role", perm))
    added = inject(rec_pos, rec_traces, bands * src_now.shape[1], cols)
    table = jnp.pad(courant, (0, 128 - courant.shape[0]))[None]
    own, outgoing = propagate(pieces, bands, chips, src_wavelet, src_pos, table, added)
    other = lax.ppermute(outgoing, "role", partner)
    return make_image(offset_lags, own, other)


def solution(mesh):
    field = P(("survey", "role"), "band", None)
    placed = (P("role", "band", None), P()) + (field,) * 4 + (P("survey", None),) * 4 + (P(),)
    return jax.shard_map(
        shards,
        mesh=mesh,
        in_specs=placed,
        out_specs=(P("survey", "role", "band", None), field, field),
        check_vma=False,
    )
```

```python
import functools

import jax
import jax.numpy as jnp
from jax import lax
from jax.experimental import pallas as pl
from jax.experimental.pallas import tpu as pltpu
from jax.sharding import PartitionSpec as P

SUB = 4
IMAGES = 4
PARTS = 5
CORES = 2

STENCIL_WEIGHTS = (-205.0 / 72.0, 8.0 / 5.0, -1.0 / 5.0, 8.0 / 315.0, -1.0 / 560.0)
F32 = jnp.float32
BF16 = jnp.bfloat16

VMEM_SPEC = pl.BlockSpec(memory_space=pltpu.VMEM)
SMEM_SPEC = pl.BlockSpec(memory_space=pltpu.SMEM)
ANY_SPEC = pl.BlockSpec(memory_space=pl.ANY)


def on_chip(value):
    return pltpu.with_memory_space_constraint(value, pltpu.VMEM)


def params(scratch_bytes):
    return pltpu.CompilerParams(vmem_limit_bytes=scratch_bytes + scratch_bytes // 4 + (4 << 20))


def split(value):
    high = value.astype(BF16)
    return high, (value - high.astype(F32)).astype(BF16)


def pack_kernel(vel_ref, sn_ref, sp_ref, rn_ref, rp_ref, pair_ref, send_ref):
    core = lax.rem(lax.axis_index("role"), CORES)
    entry = vel_ref[...].astype(F32).astype(BF16)
    src_now, rec_now = sn_ref[...], rn_ref[...]
    src_step, rec_step = src_now - sp_ref[...], rec_now - rp_ref[...]
    for out_ref, wants_source in ((pair_ref.at[0], core == 0), (send_ref, core != 0)):
        now = jnp.where(wants_source, src_now, rec_now)
        step = jnp.where(wants_source, src_step, rec_step)
        out_ref[0], out_ref[1] = split(now)
        out_ref[2], out_ref[3] = split(step)
        out_ref[4] = entry


def pack(vel_index, src_now, src_prev, rec_now, rec_prev):
    shape = (PARTS,) + src_now.shape
    return pl.pallas_call(
        pack_kernel,
        out_shape=(pltpu.VMEM((CORES,) + shape, BF16), pltpu.VMEM(shape, BF16)),
        in_specs=[VMEM_SPEC] * 5,
        out_specs=(VMEM_SPEC, VMEM_SPEC),
        compiler_params=params(0),
        name="pack",
    )(vel_index, src_now, src_prev, rec_now, rec_prev)


def inject_kernel(chunk, pos_ref, amp_ref, out_ref, acc_ref):
    count = amp_ref.shape[1]
    steps, rows, cols = out_ref.shape
    own = pl.ds(pl.multiple_of(lax.rem(lax.axis_index("role"), CORES) * steps, steps), steps)
    acc_ref[...] = jnp.zeros_like(acc_ref)

    def one(at, carry):
        span = pl.ds(pl.multiple_of(at * chunk, chunk), chunk)
        pos = pos_ref[:, span]
        in_row = lax.broadcasted_iota(jnp.int32, (rows, chunk), 0) == pos[0:1]
        in_col = lax.broadcasted_iota(jnp.int32, (cols, chunk), 0) == pos[1:2]
        col_hot = jnp.where(in_col, 1.0, 0.0).astype(BF16)
        amp = amp_ref[own, span]
        high = amp.astype(BF16).astype(F32)
        total = None
        for part in (high, amp - high):
            spread = jnp.concatenate(
                [jnp.where(in_row, part[k : k + 1], 0.0).astype(BF16) for k in range(steps)], axis=0
            )
            added = lax.dot_general(
                spread, col_hot, (((1,), (1,)), ((), ())), preferred_element_type=F32
            )
            total = added if total is None else total + added
        acc_ref[...] += total
        return carry

    lax.fori_loop(0, count // chunk, one, 0)
    for k in range(steps):
        out_ref[k] = acc_ref[k * rows : (k + 1) * rows]


def inject(rec_pos, rec_traces, rows, cols):
    count, steps = rec_traces.shape
    own_steps = steps // CORES
    chunk = next(c for c in (512, 256, 128, count) if count % c == 0)
    scratch = own_steps * rows * cols * 4
    return pl.pallas_call(
        functools.partial(inject_kernel, chunk),
        out_shape=pltpu.VMEM((own_steps, rows, cols), F32),
        in_specs=[VMEM_SPEC] * 2,
        out_specs=VMEM_SPEC,
        scratch_shapes=[pltpu.VMEM((own_steps * rows, cols), F32)],
        compiler_params=params(6 * scratch),
        name="inject",
    )(on_chip(rec_pos.T), on_chip(rec_traces.T))


def lookup(table, entry):
    width = table.shape[1]
    pieces = [
        jnp.take_along_axis(table, entry[:, at : at + width], axis=1)
        for at in range(0, entry.shape[1], width)
    ]
    return pieces[0] if len(pieces) == 1 else jnp.concatenate(pieces, axis=1)


def shift_weights(cols):
    apart = lax.broadcasted_iota(jnp.int32, (cols, cols), 0)
    apart = jnp.abs(apart - lax.broadcasted_iota(jnp.int32, (cols, cols), 1))
    weights = jnp.zeros((cols, cols), F32)
    for j in range(1, 5):
        weights = jnp.where(apart == j, STENCIL_WEIGHTS[j], weights)
    return split(weights)


def step_kernel(bands, chips, steps, *refs):
    wavelet_ref, src_pos_ref, courant_ref, late_ref, early_ref = refs[:5]
    piece_refs = refs[5 : 5 + bands * chips]
    keep_ref, send_ref = refs[5 + bands * chips : 7 + bands * chips]
    one_ref, two_ref, speed_ref, row_ref, table_ref, mix_ref, one_split, two_split = refs[
        7 + bands * chips :
    ]
    _, _, tile_z, tile_y, cols = piece_refs[0].shape
    depth, rows, _ = speed_ref.shape
    role, band = lax.axis_index("role"), lax.axis_index("band")
    core, chip = lax.rem(role, CORES), lax.div(role, CORES)
    is_source = core == 0
    sources = src_pos_ref.shape[0]
    tiles = rows // 8
    unroll = tiles * depth * cols <= 64 * 128

    for ref in (one_ref, two_ref):
        edge = jnp.zeros((rows + 16, cols), F32)
        ref[0] = edge
        ref[depth + 1] = edge
        for z in range(1, depth + 1):
            ref[z, 0:8] = edge[0:8]
            ref[z, rows + 8 :] = edge[0:8]

    high, low = shift_weights(cols)
    for at in (0, cols):
        mix_ref[at : at + cols, 0:cols] = high
        mix_ref[at : at + cols, cols:] = low

    table_ref[...] = jnp.zeros_like(table_ref)
    table_ref[:, 0 : courant_ref.shape[1]] = jnp.broadcast_to(
        courant_ref[...], (table_ref.shape[0], courant_ref.shape[1])
    )
    table = table_ref[...]
    for shift in range(bands):
        from_band = lax.rem(band + (bands - shift), bands)
        y0 = pl.multiple_of(from_band * tile_y, tile_y)
        for hop in range(chips):
            from_chip = lax.rem(chip + (chips - hop), chips)
            piece = piece_refs[shift * chips + hop]
            for part in range(CORES):
                from_core = core if part == 0 else 1 - core
                z0 = (from_chip * CORES + from_core) * tile_z
                for z in range(tile_z):
                    planes = [piece[part, k, z].astype(F32) for k in range(PARTS)]
                    now = planes[0] + planes[1]
                    one_ref[z0 + z + 1, pl.ds(y0 + 8, tile_y)] = now
                    two_ref[z0 + z + 1, pl.ds(y0 + 8, tile_y)] = now - (planes[2] + planes[3])
                    speed_ref[z0 + z, pl.ds(y0, tile_y)] = lookup(table, planes[4].astype(jnp.int32))

    lane = lax.broadcasted_iota(jnp.int32, (1, cols), 1)
    for i in range(sources):
        speed_row = speed_ref[src_pos_ref[i, 0], pl.ds(src_pos_ref[i, 1], 1)]
        row_ref[pl.ds(i, 1)] = jnp.where(lane == src_pos_ref[i, 2], speed_row, 0.0)

    def over_tiles(do):
        if unroll:
            for tile in range(tiles):
                do(tile * 8)
        else:

            def one_tile(tile, carry):
                do(pl.multiple_of(tile * 8, 8))
                return carry

            lax.fori_loop(0, tiles, one_tile, 0)

    def rows_of(y0, count):
        return pl.ds(y0 * depth if unroll else pl.multiple_of(y0 * depth, 8 * depth), count)

    def store_split(split_ref, y0, z, two_planes):
        high, low = split(two_planes)
        start = y0 * depth + z * 8
        at = pl.ds(start if unroll else pl.multiple_of(start, 16), 16)
        split_ref[at, 0:cols] = high
        split_ref[at, cols:] = low

    def beside(ref, z, y0, distance):
        if unroll:
            return ref[z + 1, pl.ds(y0 + 8 + distance, 8)]
        return ref[z + 1, pl.ds(y0, 24)][8 + distance : 16 + distance]

    def first_split(y0):
        for z in range(0, depth, 2):
            planes = [one_ref[z + k + 1, pl.ds(y0 + 8, 8)] for k in range(2)]
            store_split(one_split, y0, z, jnp.concatenate(planes, axis=0))

    over_tiles(first_split)

    def advance(now_ref, now_split, new_ref, new_split, tick):
        @pl.when(is_source)
        def _():
            for i in range(sources):
                at = (src_pos_ref[i, 0] + 1, pl.ds(src_pos_ref[i, 1] + 8, 1))
                new_ref[at] = new_ref[at] - wavelet_ref[i, tick] * row_ref[pl.ds(i, 1)]

        @pl.when(jnp.logical_not(is_source))
        def _():
            half = late_ref.shape[0]
            at = lax.rem(tick, half)
            added = jnp.where(tick < half, early_ref[at], late_ref[at])
            new_ref[1, 8 : rows + 8] = new_ref[1, 8 : rows + 8] - speed_ref[0] * added

        def stencil(y0):
            inline = lax.dot_general(
                now_split[rows_of(y0, 8 * depth)],
                mix_ref[...],
                (((1,), (0,)), ((), ())),
                preferred_element_type=F32,
            )
            inline = inline[:, 0:cols] + inline[:, cols:]
            mids = [None] * 4 + [now_ref[z + 1, pl.ds(y0 + 8, 8)] for z in range(4)]
            planes = []
            for z in range(depth):
                mids.append(now_ref[z + 5, pl.ds(y0 + 8, 8)] if z + 4 < depth else None)
                mid = mids[4]
                total = (3.0 * STENCIL_WEIGHTS[0]) * mid + inline[z * 8 : z * 8 + 8]
                for j in range(1, 5):
                    pairs = beside(now_ref, z, y0, j) + beside(now_ref, z, y0, -j)
                    for near in (mids[4 - j], mids[4 + j]):
                        if near is not None:
                            pairs = pairs + near
                    total = total + STENCIL_WEIGHTS[j] * pairs
                mids.pop(0)
                old = new_ref[z + 1, pl.ds(y0 + 8, 8)]
                new = (2.0 * mid - old) + speed_ref[z, pl.ds(y0, 8)] * total
                new_ref[z + 1, pl.ds(y0 + 8, 8)] = new
                planes.append(new)
                if len(planes) == 2:
                    store_split(new_split, y0, z - 1, jnp.concatenate(planes, axis=0))
                    planes = []

        over_tiles(stencil)

    y_own = pl.ds(pl.multiple_of(band * tile_y, tile_y) + 8, tile_y)

    def image_time(snapshot, carry):
        fields = ((one_ref, one_split), (two_ref, two_split))
        for substep in range(SUB):
            now, new = fields[substep % 2], fields[1 - substep % 2]
            advance(*now, *new, snapshot * SUB + substep)
        for out_ref, owner in ((keep_ref, role), (send_ref, chip * CORES + (1 - core))):
            for z in range(tile_z + 2):
                out_ref[snapshot, z] = fields[SUB % 2][0][owner * tile_z + z, y_own]
        return carry

    lax.fori_loop(0, steps // SUB, image_time, 0)


def propagate(pieces, bands, chips, wavelet, src_pos, courant, late, early):
    _, _, tile_z, tile_y, cols = pieces[0].shape
    depth, rows = chips * CORES * tile_z, bands * tile_y
    steps = wavelet.shape[1]
    snaps = pltpu.VMEM((steps // SUB, tile_z + 2, tile_y, cols), F32)
    field = pltpu.VMEM((depth + 2, rows + 16, cols), F32)
    parted = pltpu.VMEM((depth * rows, 2 * cols), BF16)
    scratch = 4 * cols * (2 * (depth + 2) * (rows + 16) + 3 * depth * rows + 4 * cols)
    return pl.pallas_call(
        functools.partial(step_kernel, bands, chips, steps),
        out_shape=(snaps, snaps),
        in_specs=[SMEM_SPEC] * 2 + [VMEM_SPEC] * (3 + len(pieces)),
        out_specs=(VMEM_SPEC, VMEM_SPEC),
        scratch_shapes=[
            field,
            field,
            pltpu.VMEM((depth, rows, cols), F32),
            pltpu.VMEM((max(8, src_pos.shape[0]), cols), F32),
            pltpu.VMEM((tile_y, 128), F32),
            pltpu.VMEM((2 * cols, 2 * cols), BF16),
            parted,
            parted,
        ],
        compiler_params=params(scratch),
        name="propagate",
    )(wavelet, src_pos, courant, *map(on_chip, (late, early, *pieces)))


def image_kernel(group, lag_ref, own_ref, other_ref, image_ref, src_ref, rec_ref, *scratch):
    fields_ref, sums_ref, image_sems, field_sems = scratch
    is_source = lax.rem(lax.axis_index("role"), CORES) == 0
    images, planes, tile_y, cols = own_ref.shape
    for i in range(images):
        for z in range(planes):
            own, other = own_ref[i, z], other_ref[i, z]
            fields_ref[0, i, z] = jnp.where(is_source, own, other)
            fields_ref[1, i, z] = jnp.where(is_source, other, own)
    copies = []
    for k, out_ref in enumerate((src_ref, rec_ref)):
        copies.append(
            pltpu.make_async_copy(
                fields_ref.at[k, images - 1, pl.ds(1, planes - 2)], out_ref, field_sems.at[k]
            )
        )
        copies[-1].start()
    lanes = lax.broadcasted_iota(jnp.int32, (tile_y, cols), 1)
    for slot in range(lag_ref.shape[0]):
        lag = lag_ref[slot]
        reach = jnp.abs(lag)
        there = lax.rem(2 * cols - 2 * lag, cols)
        back = lax.rem(cols + lag, cols)
        sums = []
        for z in range(planes):
            total = None
            for i in range(images):
                term = fields_ref[0, i, z] * pltpu.roll(fields_ref[1, i, z], there, 1)
                total = term if total is None else total + term
            sums.append(total)
        inside = (lanes >= reach) & (lanes < cols - reach)
        for z in range(planes - 2):
            value = (2.0 * sums[z + 1] - sums[z]) - sums[z + 2]
            sums_ref[slot, z] = jnp.where(inside, pltpu.roll(value, back, 1), 0.0).astype(BF16)
        if (slot + 1) % group == 0:
            at = pl.ds(slot + 1 - group, group)
            copies.append(
                pltpu.make_async_copy(
                    sums_ref.at[at], image_ref.at[at], image_sems.at[slot // group]
                )
            )
            copies[-1].start()
    for copy in copies:
        copy.wait()


def make_image(lags, own, other):
    images, planes, tile_y, cols = own.shape
    count = lags.shape[0]
    group = next(g for g in (8, 4, 2, 1) if count % g == 0)
    field = jax.ShapeDtypeStruct((planes - 2, tile_y, cols), F32)
    image = jax.ShapeDtypeStruct((count, planes - 2, tile_y, cols), BF16)
    return pl.pallas_call(
        functools.partial(image_kernel, group),
        out_shape=(image, field, field),
        in_specs=[SMEM_SPEC] + [VMEM_SPEC] * 2,
        out_specs=(ANY_SPEC,) * 3,
        scratch_shapes=[
            pltpu.VMEM((2,) + own.shape, F32),
            pltpu.VMEM(image.shape, BF16),
            pltpu.SemaphoreType.DMA((count // group,)),
            pltpu.SemaphoreType.DMA((2,)),
        ],
        compiler_params=params(4 * image.size),
        name="image",
    )(lags, on_chip(own), on_chip(other))


def shards(
    vel_index,
    courant,
    src_now,
    src_prev,
    rec_now,
    rec_prev,
    src_pos,
    src_wavelet,
    rec_pos,
    rec_traces,
    offset_lags,
):
    bands, roles = lax.axis_size("band"), lax.axis_size("role")
    chips = roles // CORES
    cols = src_now.shape[2]
    partner = [(i, i + 1 - 2 * (i % CORES)) for i in range(roles)]

    pair, send = pack(vel_index, src_now, src_prev, rec_now, rec_prev)
    pair = lax.dynamic_update_index_in_dim(pair, lax.ppermute(send, "role", partner), 1, 0)
    pieces = []
    for shift in range(bands):
        moved = pair
        if shift:
            moved = lax.ppermute(pair, "band", [(i, (i + shift) % bands) for i in range(bands)])
        pieces.append(moved)
        for hop in range(1, chips):
            perm = [(i, (i + CORES * hop) % roles) for i in range(roles)]
            pieces.append(lax.ppermute(moved, "role", perm))
    late = inject(rec_pos, rec_traces, bands * src_now.shape[1], cols)
    early = lax.ppermute(late, "role", [(i, i + 1) for i in range(0, roles, CORES)])
    own, outgoing = propagate(
        pieces, bands, chips, src_wavelet, src_pos, courant[None], late, early
    )
    other = lax.ppermute(outgoing, "role", partner)
    return make_image(offset_lags, own, other)


def solution(mesh):
    field = P(("survey", "role"), "band", None)
    placed = (P("role", "band", None), P()) + (field,) * 4 + (P("survey", None),) * 4 + (P(),)
    return jax.shard_map(
        shards,
        mesh=mesh,
        in_specs=placed,
        out_specs=(P("survey", "role", "band", None), field, field),
        check_vma=False,
    )
```

```python
import functools

import jax
import jax.numpy as jnp
from jax import lax
from jax.experimental import pallas as pl
from jax.experimental.pallas import tpu as pltpu
from jax.sharding import PartitionSpec as P

SUB = 4
IMAGES = 4
PARTS = 5
CORES = 2

STENCIL_WEIGHTS = (-205.0 / 72.0, 8.0 / 5.0, -1.0 / 5.0, 8.0 / 315.0, -1.0 / 560.0)
F32 = jnp.float32
BF16 = jnp.bfloat16

VMEM_SPEC = pl.BlockSpec(memory_space=pltpu.VMEM)
SMEM_SPEC = pl.BlockSpec(memory_space=pltpu.SMEM)
HBM_SPEC = pl.BlockSpec(memory_space=pltpu.HBM)
ANY_SPEC = pl.BlockSpec(memory_space=pl.ANY)


def on_chip(value):
    return pltpu.with_memory_space_constraint(value, pltpu.VMEM)


def params(scratch_bytes):
    return pltpu.CompilerParams(vmem_limit_bytes=scratch_bytes + scratch_bytes // 4 + (4 << 20))


def split(value):
    high = value.astype(BF16)
    return high, (value - high.astype(F32)).astype(BF16)


def pack_kernel(*refs):
    fields, (pos_ref, amp_ref) = refs[:5], refs[5:7]
    pair_ref, send_ref, own_pos_ref, own_amp_ref = refs[7:11]
    held, sems = refs[11:16], refs[16]
    core = lax.rem(lax.axis_index("role"), CORES)
    steps = own_amp_ref.shape[0]
    own_steps = pl.ds(pl.multiple_of(core * steps, steps), steps)
    moves = list(zip(fields, held))
    moves += [(pos_ref, own_pos_ref), (amp_ref.at[own_steps], own_amp_ref)]
    copies = [pltpu.make_async_copy(a, b, sems.at[k]) for k, (a, b) in enumerate(moves)]
    for copy in copies:
        copy.start()
    for copy in copies[:5]:
        copy.wait()
    vel_ref, sn_ref, sp_ref, rn_ref, rp_ref = held
    entry = vel_ref[...].astype(F32).astype(BF16)
    src_now, rec_now = sn_ref[...], rn_ref[...]
    src_step, rec_step = src_now - sp_ref[...], rec_now - rp_ref[...]
    for out_ref, wants_source in ((pair_ref.at[0], core == 0), (send_ref, core != 0)):
        now = jnp.where(wants_source, src_now, rec_now)
        step = jnp.where(wants_source, src_step, rec_step)
        out_ref[0], out_ref[1] = split(now)
        out_ref[2], out_ref[3] = split(step)
        out_ref[4] = entry
    for copy in copies[5:]:
        copy.wait()


def pack(vel_index, src_now, src_prev, rec_now, rec_prev, rec_pos, rec_traces):
    shape = (PARTS,) + src_now.shape
    count, steps = rec_traces.shape
    held = pltpu.VMEM(src_now.shape, F32)
    return pl.pallas_call(
        pack_kernel,
        out_shape=(
            pltpu.VMEM((CORES,) + shape, BF16),
            pltpu.VMEM(shape, BF16),
            pltpu.VMEM((2, count), jnp.int32),
            pltpu.VMEM((steps // CORES, count), F32),
        ),
        in_specs=[HBM_SPEC] * 7,
        out_specs=(VMEM_SPEC,) * 4,
        scratch_shapes=[pltpu.VMEM(src_now.shape, jnp.int32)]
        + [held] * 4
        + [pltpu.SemaphoreType.DMA((7,))],
        compiler_params=params(0),
        name="pack",
    )(vel_index, src_now, src_prev, rec_now, rec_prev, rec_pos.T, rec_traces.T)


def inject_kernel(chunk, pos_ref, amp_ref, out_ref, acc_ref):
    count = amp_ref.shape[1]
    steps, rows, cols = out_ref.shape
    acc_ref[...] = jnp.zeros_like(acc_ref)

    def one(at, carry):
        span = pl.ds(pl.multiple_of(at * chunk, chunk), chunk)
        pos = pos_ref[:, span]
        in_row = lax.broadcasted_iota(jnp.int32, (rows, chunk), 0) == pos[0:1]
        in_col = lax.broadcasted_iota(jnp.int32, (cols, chunk), 0) == pos[1:2]
        col_hot = jnp.where(in_col, 1.0, 0.0).astype(BF16)
        amp = amp_ref[:, span]
        high = amp.astype(BF16).astype(F32)
        total = None
        for part in (high, amp - high):
            spread = jnp.concatenate(
                [jnp.where(in_row, part[k : k + 1], 0.0).astype(BF16) for k in range(steps)], axis=0
            )
            added = lax.dot_general(
                spread, col_hot, (((1,), (1,)), ((), ())), preferred_element_type=F32
            )
            total = added if total is None else total + added
        acc_ref[...] += total
        return carry

    lax.fori_loop(0, count // chunk, one, 0)
    for k in range(steps):
        out_ref[k] = acc_ref[k * rows : (k + 1) * rows]


def inject(own_pos, own_amp, rows, cols):
    steps, count = own_amp.shape
    chunk = next(c for c in (512, 256, 128, count) if count % c == 0)
    scratch = steps * rows * cols * 4
    return pl.pallas_call(
        functools.partial(inject_kernel, chunk),
        out_shape=pltpu.VMEM((steps, rows, cols), F32),
        in_specs=[VMEM_SPEC] * 2,
        out_specs=VMEM_SPEC,
        scratch_shapes=[pltpu.VMEM((steps * rows, cols), F32)],
        compiler_params=params(6 * scratch),
        name="inject",
    )(on_chip(own_pos), on_chip(own_amp))


def across(at, shift, count):
    return at ^ shift if count & (count - 1) == 0 else (at + count - shift) % count


def lookup(table, entry):
    width = table.shape[1]
    pieces = [
        jnp.take_along_axis(table, entry[:, at : at + width], axis=1)
        for at in range(0, entry.shape[1], width)
    ]
    return pieces[0] if len(pieces) == 1 else jnp.concatenate(pieces, axis=1)


def shift_weights(cols):
    apart = lax.broadcasted_iota(jnp.int32, (cols, cols), 0)
    apart = jnp.abs(apart - lax.broadcasted_iota(jnp.int32, (cols, cols), 1))
    weights = jnp.zeros((cols, cols), F32)
    for j in range(1, 5):
        weights = jnp.where(apart == j, STENCIL_WEIGHTS[j], weights)
    return split(weights)


def step_kernel(bands, chips, steps, *refs):
    wavelet_ref, src_pos_ref, courant_ref, late_ref, early_ref = refs[:5]
    piece_refs = refs[5 : 5 + bands * chips]
    keep_ref, send_ref = refs[5 + bands * chips : 7 + bands * chips]
    one_ref, two_ref, speed_ref, row_ref, table_ref, mix_ref, parts_ref, inline_ref = refs[
        7 + bands * chips :
    ]
    _, _, tile_z, tile_y, cols = piece_refs[0].shape
    depth, rows, _ = speed_ref.shape
    role, band = lax.axis_index("role"), lax.axis_index("band")
    core, chip = lax.rem(role, CORES), lax.div(role, CORES)
    is_source = core == 0
    sources = src_pos_ref.shape[0]
    tiles = rows // 8
    unroll = tiles * depth * cols <= 64 * 128

    for ref in (one_ref, two_ref):
        edge = jnp.zeros((rows + 16, cols), F32)
        ref[0] = edge
        ref[depth + 1] = edge
        for z in range(1, depth + 1):
            ref[z, 0:8] = edge[0:8]
            ref[z, rows + 8 :] = edge[0:8]

    high, low = shift_weights(cols)
    for at in (0, cols):
        mix_ref[at : at + cols, 0:cols] = high
        mix_ref[at : at + cols, cols:] = low

    table_ref[...] = jnp.zeros_like(table_ref)
    table_ref[:, 0 : courant_ref.shape[1]] = jnp.broadcast_to(
        courant_ref[...], (table_ref.shape[0], courant_ref.shape[1])
    )
    table = table_ref[...]
    for shift in range(bands):
        from_band = across(band, shift, bands)
        y0 = pl.multiple_of(from_band * tile_y, tile_y)
        for hop in range(chips):
            from_chip = lax.rem(chip + (chips - hop), chips)
            piece = piece_refs[shift * chips + hop]
            for part in range(CORES):
                from_core = core if part == 0 else 1 - core
                z0 = (from_chip * CORES + from_core) * tile_z
                for z in range(tile_z):
                    planes = [piece[part, k, z].astype(F32) for k in range(PARTS)]
                    now = planes[0] + planes[1]
                    one_ref[z0 + z + 1, pl.ds(y0 + 8, tile_y)] = now
                    two_ref[z0 + z + 1, pl.ds(y0 + 8, tile_y)] = now - (planes[2] + planes[3])
                    speed_ref[z0 + z, pl.ds(y0, tile_y)] = lookup(table, planes[4].astype(jnp.int32))

    lane = lax.broadcasted_iota(jnp.int32, (1, cols), 1)
    for i in range(sources):
        speed_row = speed_ref[src_pos_ref[i, 0], pl.ds(src_pos_ref[i, 1], 1)]
        row_ref[pl.ds(i, 1)] = jnp.where((lane == src_pos_ref[i, 2]) & is_source, speed_row, 0.0)

    def over_tiles(do):
        if unroll:
            for tile in range(tiles):
                do(tile * 8)
        else:

            def one_tile(tile, carry):
                do(pl.multiple_of(tile * 8, 8))
                return carry

            lax.fori_loop(0, tiles, one_tile, 0)

    def rows_of(y0, z, planes):
        start = y0 * depth + z * 8
        return pl.ds(start if unroll else pl.multiple_of(start, 8), planes * 8)

    def store_parts(z, two_planes):
        high, low = split(two_planes)
        parts_ref[z * 8 : z * 8 + 16, 0:cols] = high
        parts_ref[z * 8 : z * 8 + 16, cols:] = low

    def sum_inline(y0):
        sums = lax.dot_general(
            parts_ref[...], mix_ref[...], (((1,), (0,)), ((), ())), preferred_element_type=F32
        )
        inline_ref[rows_of(y0, 0, depth)] = sums[:, 0:cols] + sums[:, cols:]

    def beside(ref, z, y0, distance):
        if unroll:
            return ref[z + 1, pl.ds(y0 + 8 + distance, 8)]
        return ref[z + 1, pl.ds(y0, 24)][8 + distance : 16 + distance]

    def first_inline(y0):
        for z in range(0, depth, 2):
            planes = [one_ref[z + k + 1, pl.ds(y0 + 8, 8)] for k in range(2)]
            store_parts(z, jnp.concatenate(planes, axis=0))
        sum_inline(y0)

    over_tiles(first_inline)

    def advance(now_ref, new_ref, tick):
        half = late_ref.shape[0]
        turn = lax.rem(tick, half)
        added = jnp.where(tick < half, early_ref[turn], late_ref[turn])
        added = jnp.where(is_source, 0.0, speed_ref[0] * added)
        new_ref[1, 8 : rows + 8] = new_ref[1, 8 : rows + 8] - added
        for i in range(sources):
            at = (src_pos_ref[i, 0] + 1, pl.ds(src_pos_ref[i, 1] + 8, 1))
            new_ref[at] = new_ref[at] - wavelet_ref[i, tick] * row_ref[pl.ds(i, 1)]

        def stencil(y0):
            mids = [None] * 4 + [now_ref[z + 1, pl.ds(y0 + 8, 8)] for z in range(4)]
            planes = []
            for z in range(depth):
                mids.append(now_ref[z + 5, pl.ds(y0 + 8, 8)] if z + 4 < depth else None)
                mid = mids[4]
                total = (3.0 * STENCIL_WEIGHTS[0]) * mid + inline_ref[rows_of(y0, z, 1)]
                for j in range(1, 5):
                    pairs = beside(now_ref, z, y0, j) + beside(now_ref, z, y0, -j)
                    for near in (mids[4 - j], mids[4 + j]):
                        if near is not None:
                            pairs = pairs + near
                    total = total + STENCIL_WEIGHTS[j] * pairs
                mids.pop(0)
                old = new_ref[z + 1, pl.ds(y0 + 8, 8)]
                new = (2.0 * mid - old) + speed_ref[z, pl.ds(y0, 8)] * total
                new_ref[z + 1, pl.ds(y0 + 8, 8)] = new
                planes.append(new)
                if len(planes) == 2:
                    store_parts(z - 1, jnp.concatenate(planes, axis=0))
                    planes = []
            sum_inline(y0)

        over_tiles(stencil)

    y_own = pl.ds(pl.multiple_of(band * tile_y, tile_y) + 8, tile_y)

    def image_time(snapshot, carry):
        fields = (one_ref, two_ref)
        for substep in range(SUB):
            now_ref, new_ref = fields[substep % 2], fields[1 - substep % 2]
            advance(now_ref, new_ref, snapshot * SUB + substep)
        for out_ref, owner in ((keep_ref, role), (send_ref, chip * CORES + (1 - core))):
            for z in range(tile_z + 2):
                out_ref[snapshot, z] = fields[SUB % 2][owner * tile_z + z, y_own]
        return carry

    lax.fori_loop(0, steps // SUB, image_time, 0)


def propagate(pieces, bands, chips, wavelet, src_pos, courant, late, early):
    _, _, tile_z, tile_y, cols = pieces[0].shape
    depth, rows = chips * CORES * tile_z, bands * tile_y
    steps = wavelet.shape[1]
    snaps = pltpu.VMEM((steps // SUB, tile_z + 2, tile_y, cols), F32)
    field = pltpu.VMEM((depth + 2, rows + 16, cols), F32)
    scratch = 4 * cols * (2 * (depth + 2) * (rows + 16) + 3 * depth * rows + 4 * cols)
    return pl.pallas_call(
        functools.partial(step_kernel, bands, chips, steps),
        out_shape=(snaps, snaps),
        in_specs=[SMEM_SPEC] * 2 + [VMEM_SPEC] * (3 + len(pieces)),
        out_specs=(VMEM_SPEC, VMEM_SPEC),
        scratch_shapes=[
            field,
            field,
            pltpu.VMEM((depth, rows, cols), F32),
            pltpu.VMEM((max(8, src_pos.shape[0]), cols), F32),
            pltpu.VMEM((tile_y, 128), F32),
            pltpu.VMEM((2 * cols, 2 * cols), BF16),
            pltpu.VMEM((depth * 8, 2 * cols), BF16),
            pltpu.VMEM((depth * rows, cols), F32),
        ],
        compiler_params=params(scratch),
        name="propagate",
    )(wavelet, src_pos, courant, *map(on_chip, (late, early, *pieces)))


def image_kernel(group, lag_ref, own_ref, other_ref, image_ref, src_ref, rec_ref, *scratch):
    fields_ref, parts_ref, sums_ref, image_sems, field_sems = scratch
    is_source = lax.rem(lax.axis_index("role"), CORES) == 0
    images, planes, tile_y, cols = own_ref.shape
    for i in range(images):
        for z in range(planes):
            own, other = own_ref[i, z], other_ref[i, z]
            fields_ref[0, i, z] = jnp.where(is_source, own, other)
            fields_ref[1, i, z] = jnp.where(is_source, other, own)
    copies = []
    for k, out_ref in enumerate((src_ref, rec_ref)):
        copies.append(
            pltpu.make_async_copy(
                fields_ref.at[k, images - 1, pl.ds(1, planes - 2)], out_ref, field_sems.at[k]
            )
        )
        copies[-1].start()
    high, low = split(fields_ref[1].reshape(images * planes * tile_y, cols))
    parts_ref[:, 0:cols] = high
    parts_ref[:, cols:] = low
    ahead = lax.broadcasted_iota(jnp.int32, (cols, cols), 0)
    ahead = ahead - lax.broadcasted_iota(jnp.int32, (cols, cols), 1)
    for first in range(0, lag_ref.shape[0], 2):
        slots = (first, first + 1)
        moves = [jnp.where(ahead == 2 * lag_ref[h], 1.0, 0.0).astype(BF16) for h in slots]
        moves = jnp.concatenate(moves, axis=1)
        moved = lax.dot_general(
            parts_ref[...],
            jnp.concatenate([moves, moves], axis=0),
            (((1,), (0,)), ((), ())),
            preferred_element_type=F32,
        )
        for at, slot in enumerate(slots):
            sums = []
            for z in range(planes):
                total = None
                for i in range(images):
                    row = (i * planes + z) * tile_y
                    ahead_of = moved[row : row + tile_y, at * cols : (at + 1) * cols]
                    term = fields_ref[0, i, z] * ahead_of
                    total = term if total is None else total + term
                sums.append(total)
            back = lax.rem(cols + lag_ref[slot], cols)
            for z in range(planes - 2):
                value = (2.0 * sums[z + 1] - sums[z]) - sums[z + 2]
                sums_ref[slot, z] = pltpu.roll(value, back, 1).astype(BF16)
            if (slot + 1) % group == 0:
                span = pl.ds(slot + 1 - group, group)
                copies.append(
                    pltpu.make_async_copy(
                        sums_ref.at[span], image_ref.at[span], image_sems.at[slot // group]
                    )
                )
                copies[-1].start()
    for copy in copies:
        copy.wait()


def make_image(lags, own, other):
    images, planes, tile_y, cols = own.shape
    count = lags.shape[0]
    group = next(g for g in (8, 4, 2, 1) if count % g == 0)
    field = jax.ShapeDtypeStruct((planes - 2, tile_y, cols), F32)
    image = jax.ShapeDtypeStruct((count, planes - 2, tile_y, cols), BF16)
    return pl.pallas_call(
        functools.partial(image_kernel, group),
        out_shape=(image, field, field),
        in_specs=[SMEM_SPEC] + [VMEM_SPEC] * 2,
        out_specs=(ANY_SPEC,) * 3,
        scratch_shapes=[
            pltpu.VMEM((2,) + own.shape, F32),
            pltpu.VMEM((images * planes * tile_y, 2 * cols), BF16),
            pltpu.VMEM(image.shape, BF16),
            pltpu.SemaphoreType.DMA((count // group,)),
            pltpu.SemaphoreType.DMA((2,)),
        ],
        compiler_params=params(4 * image.size + 64 * cols * cols),
        name="image",
    )(lags, on_chip(own), on_chip(other))


def shards(
    vel_index,
    courant,
    src_now,
    src_prev,
    rec_now,
    rec_prev,
    src_pos,
    src_wavelet,
    rec_pos,
    rec_traces,
    offset_lags,
):
    bands, roles = lax.axis_size("band"), lax.axis_size("role")
    chips = roles // CORES
    cols = src_now.shape[2]
    partner = [(i, i + 1 - 2 * (i % CORES)) for i in range(roles)]

    pair, send, own_pos, own_amp = pack(
        vel_index, src_now, src_prev, rec_now, rec_prev, rec_pos, rec_traces
    )
    pair = lax.dynamic_update_index_in_dim(pair, lax.ppermute(send, "role", partner), 1, 0)
    pieces = []
    for shift in range(bands):
        moved = pair
        if shift:
            swap = [(across(i, shift, bands), i) for i in range(bands)]
            moved = lax.ppermute(pair, "band", swap)
        pieces.append(moved)
        for hop in range(1, chips):
            perm = [(i, (i + CORES * hop) % roles) for i in range(roles)]
            pieces.append(lax.ppermute(moved, "role", perm))
    late = inject(own_pos, own_amp, bands * src_now.shape[1], cols)
    early = lax.ppermute(late, "role", [(i, i + 1) for i in range(0, roles, CORES)])
    own, outgoing = propagate(
        pieces, bands, chips, src_wavelet, src_pos, courant[None], late, early
    )
    other = lax.ppermute(outgoing, "role", partner)
    return make_image(offset_lags, own, other)


def solution(mesh):
    field = P(("survey", "role"), "band", None)
    placed = (P("role", "band", None), P()) + (field,) * 4 + (P("survey", None),) * 4 + (P(),)
    return jax.shard_map(
        shards,
        mesh=mesh,
        in_specs=placed,
        out_specs=(P("survey", "role", "band", None), field, field),
        check_vma=False,
    )
```
